32 devices in a mesh: row: 2 (over x), col: 16 (over z, y, core).
Axes of the slice: x: 2, y: 2, z: 4, core: 2. Of those that a mesh axis runs over, the one named last changes fastest.
Arguments:
- features: bfloat16 [64, 768, 256], P('row', 'col'), may hold values from -6 to 6
- conv_one: bfloat16 [3, 3, 256, 256], replicated, may hold values from -0.125 to 0.125
- bias_one: float32 [256], replicated, may hold values from -3 to 3
- conv_two: bfloat16 [3, 3, 256, 512], replicated, may hold values from -0.125 to 0.125
- bias_two: float32 [512], replicated, may hold values from -3 to 3
- conv_three: bfloat16 [16, 3, 3, 32, 32], P('col'), may hold values from -0.375 to 0.375
- bias_three: float32 [512], P('col'), may hold values from -3 to 3
Outputs:
- encoded: bfloat16 [32, 512, 384], P('row', 'col')
The draws below stay inside these ranges and needn't reach their ends.
All inputs are finite; a program needn't handle non-finite values.
Results may differ from the reference program's by a relative error of at most 0.0051.
Values may be sent and summed in bfloat16 or wider, within the bound.
A program may use at most 64 MiB of HBM per device.

```python
import jax
import jax.numpy as jnp
from jax import lax

C1 = 256
C2 = 512
GROUPS = 16
GW = 32
H1 = 64
W1 = 768


def block_scale(own_key, dims, pieces, low, top_value):
    level, own = 1.0, jax.random.fold_in(own_key, 6)
    for dim, parts in pieces:
        steps = jnp.exp(jax.random.uniform(jax.random.fold_in(own, dim), (parts,), jnp.float32, low / len(pieces), top_value / len(pieces)))
        level = level * jnp.repeat(steps, dims[dim] // parts).reshape([-1 if axis == dim else 1 for axis in range(len(dims))])
    return level


def gaussian(rng, shape, scale, limit, shards=(), dtype=jnp.bfloat16):
    result = scale * jax.random.normal(rng, shape, jnp.float32)
    if shards:
        result = result * block_scale(rng, shape, shards, -0.22, 0.18)
    return jnp.clip(result, -limit, limit).astype(dtype)


def setup_inputs(seed: int = 0) -> dict:
    splits = jax.random.split(jax.random.key(seed), 8)
    features = gaussian(splits[0], (H1, W1, C1), 1.0, 6.0, ((0, 2), (1, 16)))
    conv_one = gaussian(splits[1], (3, 3, C1, C1), (9 * C1) ** -0.5, 0.125)
    bias_one = gaussian(splits[2], (C1,), 0.5, 3.0, (), jnp.float32)
    conv_two = gaussian(splits[3], (3, 3, C1, C2), (9 * C1) ** -0.5, 0.125)
    bias_two = gaussian(splits[4], (C2,), 0.5, 3.0, (), jnp.float32)
    conv_three = gaussian(splits[5], (GROUPS, 3, 3, GW, GW), (9 * GW) ** -0.5, 0.375, ((0, 16),))
    bias_three = gaussian(splits[6], (C2,), 0.5, 3.0, ((0, 16),), jnp.float32)
    return {"features": features, "conv_one": conv_one, "bias_one": bias_one, "conv_two": conv_two, "bias_two": bias_two, "conv_three": conv_three, "bias_three": bias_three}


def convolve(inputs, kernel, stride, groups):
    return lax.conv_general_dilated(inputs, kernel, (stride, stride), ((1, 1), (1, 1)), dimension_numbers=("NHWC", "HWIO", "NHWC"), feature_group_count=groups, precision=lax.Precision.HIGHEST)


def reference(features, conv_one, bias_one, conv_two, bias_two, conv_three, bias_three):
    inputs = features.astype(jnp.float32)[None]
    summed = convolve(inputs, conv_one.astype(jnp.float32), 1, 1)
    layer_one = jax.nn.relu(summed + bias_one.astype(jnp.float32)).astype(jnp.bfloat16)
    summed = convolve(layer_one.astype(jnp.float32), conv_two.astype(jnp.float32), 2, 1)
    layer_two = jax.nn.relu(summed + bias_two.astype(jnp.float32)).astype(jnp.bfloat16)
    kernel = jnp.transpose(conv_three.astype(jnp.float32), (1, 2, 3, 0, 4)).reshape(3, 3, GW, GROUPS * GW)
    summed = convolve(layer_two.astype(jnp.float32), kernel, 1, GROUPS)
    summed = summed[0] + bias_three.astype(jnp.float32)
    return jnp.transpose(summed, (0, 2, 1)).astype(jnp.bfloat16)
```

```python
import functools

import jax
import jax.numpy as jnp
from jax import lax
from jax.experimental import pallas as pl
from jax.experimental.pallas import tpu as pltpu
from jax.sharding import PartitionSpec as P

MESH = pl.DeviceIdType.MESH
F32 = jnp.float32
BF16 = jnp.bfloat16


def dot(a, b):
    return jnp.dot(a, b, preferred_element_type=F32)


def kernel(
    rows, cols,
    feat, w1_hbm, b1, w2_hbm, b2, w3, b3, out,
    w1, w2, x32, st_l, st_r, rc_l, rc_r, rc_u, rc_d, taps, a2, l2, send, main, top, bot, l32, band,
    w_sem, h_send, h_recv, m_send, m_recv, t_send, t_recv, b_send, b_recv,
):
    row = lax.axis_index("row")
    col = lax.axis_index("col")
    tr, tc, ch = feat.shape
    half = tc // 2
    has_up, has_down = row > 0, row < rows - 1
    has_left, has_right = col > 0, col < cols - 1

    load_one = pltpu.make_async_copy(w1_hbm, w1, w_sem.at[0])
    load_two = pltpu.make_async_copy(w2_hbm, w2, w_sem.at[1])
    load_one.start()
    load_two.start()

    barrier = pltpu.get_barrier_semaphore()

    def greet(device_row, first):
        def body(k, carry):
            pl.semaphore_signal(
                barrier, inc=1, device_id=(device_row, lax.rem(col + k, cols)), device_id_type=MESH
            )
            return carry

        lax.fori_loop(first, cols, body, 0)

    greet(row, 1)
    pl.when(has_up)(lambda: greet(row - 1, 0))
    pl.when(has_down)(lambda: greet(row + 1, 0))

    lanes_of = [slice(128 * h, 128 * h + 128) for h in range(ch // 128)]
    for h, part in enumerate(lanes_of):
        x32[h, 2 : tr + 2, 8 : tc + 8, :] = feat[:, :, part].astype(F32)
        st_r[:, :, part] = x32[h, 2 : tr + 2, tc + 6 : tc + 8, :].astype(BF16)
        st_l[:, :, part] = x32[h, 2 : tr + 2, 8:10, :].astype(BF16)
    zero = lambda ref, lo, hi: ref.__setitem__(
        slice(lo, hi), jnp.zeros((hi - lo,) + ref.shape[1:], ref.dtype)
    )
    copies = []
    plan = (
        (feat.at[tr - 2 : tr], rc_u, 1, 0, has_down, has_up, (rc_u, 0, 2)),
        (feat.at[0:1], rc_d, -1, 0, has_up, has_down, (rc_d, 0, 1)),
        (st_r, rc_l.at[2 : tr + 2], 0, 1, has_right, has_left, (rc_l, 2, tr + 2)),
        (st_l, rc_r.at[2 : tr + 2], 0, -1, has_left, has_right, (rc_r, 2, tr + 2)),
        (st_r.at[tr - 2 : tr], rc_l.at[0:2], 1, 1, has_down & has_right, has_up & has_left, (rc_l, 0, 2)),
        (st_r.at[0:1], rc_l.at[tr + 2 : tr + 3], -1, 1, has_up & has_right, has_down & has_left, (rc_l, tr + 2, tr + 3)),
        (st_l.at[tr - 2 : tr], rc_r.at[0:2], 1, -1, has_down & has_left, has_up & has_right, (rc_r, 0, 2)),
        (st_l.at[0:1], rc_r.at[tr + 2 : tr + 3], -1, -1, has_up & has_left, has_down & has_right, (rc_r, tr + 2, tr + 3)),
    )
    for index, (src, dst, dr, dc, sends, gets, hole) in enumerate(plan):
        copy = pltpu.make_async_remote_copy(
            src_ref=src, dst_ref=dst, send_sem=h_send.at[index], recv_sem=h_recv.at[index],
            device_id=(row + dr, col + dc), device_id_type=MESH,
        )
        copies.append(copy)
        pl.when(jnp.logical_not(gets))(functools.partial(zero, *hole))

    reach = cols * (1 + has_up.astype(jnp.int32) + has_down.astype(jnp.int32)) - 1
    pl.semaphore_wait(barrier, reach)
    for copy, item in zip(copies, plan):
        pl.when(item[4])(copy.start)

    width = w3.shape[3]
    quad = 4 * width
    band[...] = jnp.zeros_like(band)
    for b in range(3):
        for a in range(3):
            block = w3[0, a, b]
            for i in range(4):
                at = (i + 3 + a) * width
                band[b, at : at + width, i * width : (i + 1) * width] = block
    bias3 = jnp.concatenate([b3[...]] * 4, axis=1)
    l32[0:8, :] = jnp.zeros((8, l32.shape[1]), F32)
    full = cols * half
    l32[full + 8 : full + 16, :] = jnp.zeros((8, l32.shape[1]), F32)

    @pl.when(jnp.logical_not(has_up))
    def _():
        top[...] = jnp.zeros_like(top)

    @pl.when(jnp.logical_not(has_down))
    def _():
        bot[...] = jnp.zeros_like(bot)

    for copy, item in zip(copies, plan):
        pl.when(item[5])(copy.wait_recv)
    for h, part in enumerate(lanes_of):
        x32[h, 0:2, 8 : tc + 8, :] = rc_u[:, :, part].astype(F32)
        x32[h, tr + 2 : tr + 3, 8 : tc + 8, :] = rc_d[:, :, part].astype(F32)
        x32[h, 0 : tr + 3, 6:8, :] = rc_l[:, :, part].astype(F32)
        x32[h, 0 : tr + 3, tc + 8 : tc + 10, :] = rc_r[:, :, part].astype(F32)

    for j in range(4):
        for r in range(0, tr + 4, 12):
            for h in range(ch // 128):
                taps[r : r + 12, :, j * ch + 128 * h : j * ch + 128 * h + 128] = x32[
                    h, r : r + 12, pl.ds(j + 6, 32, stride=2), :
                ].astype(BF16)

    load_one.wait()
    bias1 = b1[...]
    left_edge = jnp.logical_not(has_left)
    for first, pairs in ((0, 8), (8, tr // 2 - 7)):
        m = pairs * 64
        for parity in range(2):
            acc = None
            for a in range(3):
                lhs = taps[2 * first + a : 2 * first + a + 2 * pairs, :, parity * ch : (parity + 3) * ch]
                part = dot(lhs.reshape(m, 3 * ch), w1[a].reshape(3 * ch, ch))
                acc = part if acc is None else acc + part
            acc = jnp.maximum(acc + bias1, 0.0)
            if parity == 0:
                spot = lax.broadcasted_iota(jnp.int32, acc.shape, 0)
                acc = jnp.where((lax.rem(spot, 32) == 0) & left_edge, 0.0, acc)
                moved = pltpu.roll(acc, m - 1, 0)
                a2[first : first + pairs, :, :, 2 * ch : 3 * ch] = moved.astype(BF16).reshape(pairs, 2, 32, ch)
            a2[first : first + pairs, :, :, parity * ch : (parity + 1) * ch] = acc.astype(BF16).reshape(
                pairs, 2, 32, ch
            )

    @pl.when(jnp.logical_not(has_up))
    def _():
        a2[0, 0] = jnp.zeros(a2.shape[2:], BF16)

    load_two.wait()
    out_ch = w2.shape[3]
    orow = tr // 2
    acc = None
    for a in range(3):
        lhs = a2[a // 2 : a // 2 + orow, a % 2].reshape(orow * 32, 3 * ch)
        part = dot(lhs, w2[a].reshape(3 * ch, out_ch))
        acc = part if acc is None else acc + part
    l2[...] = jnp.maximum(acc + b2[...], 0.0).reshape(orow, 32, out_ch)

    for q in range(orow // 4):
        for g in range(cols):
            piece = jnp.concatenate(
                [l2[4 * q + r, 0:half, g * width : (g + 1) * width] for r in range(4)], axis=1
            )
            send[g, :, q * quad : (q + 1) * quad] = piece.astype(BF16)

    span = orow * width

    def main_copy(k):
        d = lax.rem(col + k, cols)
        return pltpu.make_async_remote_copy(
            src_ref=send.at[d], dst_ref=main.at[col], send_sem=m_send.at[k], recv_sem=m_recv.at[col],
            device_id=(row, d), device_id_type=MESH,
        )

    def main_arrival(k):
        s = lax.rem(col + k, cols)
        return pltpu.make_async_remote_copy(
            src_ref=send.at[s], dst_ref=main.at[s], send_sem=m_send.at[k], recv_sem=m_recv.at[s],
            device_id=(row, s), device_id_type=MESH,
        )

    def edge_copy(k, dr):
        d = lax.rem(col + k, cols)
        lanes = pl.ds(span - quad, quad) if dr > 0 else pl.ds(0, quad)
        there, ss, rs = (top, t_send, t_recv) if dr > 0 else (bot, b_send, b_recv)
        return pltpu.make_async_remote_copy(
            src_ref=send.at[d, :, lanes], dst_ref=there.at[col], send_sem=ss.at[k], recv_sem=rs.at[col],
            device_id=(row + dr, d), device_id_type=MESH,
        )

    def edge_arrival(k, dr):
        s = lax.rem(col + k, cols)
        there, ss, rs = (top, t_send, t_recv) if dr > 0 else (bot, b_send, b_recv)
        return pltpu.make_async_remote_copy(
            src_ref=there.at[s], dst_ref=there.at[s], send_sem=ss.at[k], recv_sem=rs.at[s],
            device_id=(row - dr, s), device_id_type=MESH,
        )

    def each(first, act):
        def body(k, carry):
            act(k)
            return carry

        lax.fori_loop(first, cols, body, 0)

    each(1, lambda k: main_copy(k).start())
    pl.when(has_down)(lambda: each(0, lambda k: edge_copy(k, 1).start()))
    pl.when(has_up)(lambda: each(0, lambda k: edge_copy(k, -1).start()))
    main[col] = send[col]
    each(1, lambda k: main_arrival(k).wait_recv())
    pl.when(has_up)(lambda: each(0, lambda k: edge_arrival(k, 1).wait_recv()))
    pl.when(has_down)(lambda: each(0, lambda k: edge_arrival(k, -1).wait_recv()))

    for s in range(cols):
        at = 8 + half * s
        l32[at : at + half, 0:quad] = top[s].astype(F32)
        l32[at : at + half, quad : quad + span] = main[s].astype(F32)
        l32[at : at + half, quad + span : 2 * quad + span] = bot[s].astype(F32)

    shifted = [l32[7 + b : 7 + b + full, :].astype(BF16) for b in range(3)]
    for q in range(orow // 4):
        acc = None
        for b in range(3):
            part = dot(shifted[b][:, q * quad : (q + 3) * quad], band[b])
            acc = part if acc is None else acc + part
        out[4 * q : 4 * q + 4] = (acc + bias3).T.reshape(4, width, full).astype(BF16)

    for copy, item in zip(copies, plan):
        pl.when(item[4])(copy.wait_send)
    each(1, lambda k: main_copy(k).wait_send())
    pl.when(has_down)(lambda: each(0, lambda k: edge_copy(k, 1).wait_send()))
    pl.when(has_up)(lambda: each(0, lambda k: edge_copy(k, -1).wait_send()))


def on_device(rows, cols, features, conv_one, bias_one, conv_two, bias_two, conv_three, bias_three):
    tr, tc, ch = features.shape
    c2 = conv_two.shape[3]
    width = conv_three.shape[3]
    half, orow = tc // 2, tr // 2
    full, span, quad = cols * half, orow * width, 4 * width
    vmem = pl.BlockSpec(memory_space=pltpu.VMEM)
    hbm = pl.BlockSpec(memory_space=pl.ANY)
    dma = pltpu.SemaphoreType.DMA
    return pl.pallas_call(
        functools.partial(kernel, rows, cols),
        out_shape=jax.ShapeDtypeStruct((orow, width, full), BF16),
        in_specs=[vmem, hbm, vmem, hbm, vmem, vmem, vmem],
        out_specs=vmem,
        scratch_shapes=[
            pltpu.VMEM(conv_one.shape, BF16),
            pltpu.VMEM(conv_two.shape, BF16),
            pltpu.VMEM((ch // 128, tr + 4, tc + 24, 128), F32),
            pltpu.VMEM((tr, 2, ch), BF16),
            pltpu.VMEM((tr, 2, ch), BF16),
            pltpu.VMEM((tr + 3, 2, ch), BF16),
            pltpu.VMEM((tr + 3, 2, ch), BF16),
            pltpu.VMEM((2, tc, ch), BF16),
            pltpu.VMEM((1, tc, ch), BF16),
            pltpu.VMEM((tr + 4, 32, 4 * ch), BF16),
            pltpu.VMEM((orow + 1, 2, 32, 3 * ch), BF16),
            pltpu.VMEM((orow, 32, c2), F32),
            pltpu.VMEM((cols, half, span), BF16),
            pltpu.VMEM((cols, half, span), BF16),
            pltpu.VMEM((cols, half, quad), BF16),
            pltpu.VMEM((cols, half, quad), BF16),
            pltpu.VMEM((full + 16, span + 2 * quad), F32),
            pltpu.VMEM((3, 3 * quad, quad), BF16),
            dma((2,)), dma((8,)), dma((8,)),
            dma((cols,)), dma((cols,)), dma((cols,)), dma((cols,)), dma((cols,)), dma((cols,)),
        ],
        compiler_params=pltpu.CompilerParams(
            collective_id=0, has_side_effects=True, vmem_limit_bytes=60 * 1024 * 1024
        ),
    )(
        features, conv_one, bias_one.reshape(1, -1), conv_two, bias_two.reshape(1, -1),
        conv_three, bias_three.reshape(1, -1),
    )


def solution(mesh):
    in_specs = (
        P("row", "col", None),
        P(),
        P(),
        P(),
        P(),
        P("col", None, None, None, None),
        P("col"),
    )
    return jax.shard_map(
        functools.partial(on_device, mesh.shape["row"], mesh.shape["col"]),
        mesh=mesh, in_specs=in_specs, out_specs=P("row", "col", None), check_vma=False,
    )
```

```python
import functools

import jax
import jax.numpy as jnp
from jax import lax
from jax.experimental import pallas as pl
from jax.experimental.pallas import tpu as pltpu
from jax.sharding import PartitionSpec as P

MESH = pl.DeviceIdType.MESH
F32 = jnp.float32
BF16 = jnp.bfloat16


def dot(a, b):
    return jnp.dot(a, b, preferred_element_type=F32)


def kernel(
    rows, cols,
    feat, w1_hbm, b1, w2_hbm, b2, w3, b3, out,
    w1, w2, x32, st_l, st_r, rc_l, rc_r, rc_u, rc_d, taps, a2, l2, send, low, high, main, top, bot, l32, band,
    w_sem, h_send, h_recv, m_send, m_recv, t_send, t_recv, b_send, b_recv,
):
    row = lax.axis_index("row")
    col = lax.axis_index("col")
    tr, tc, ch = feat.shape
    half = tc // 2
    has_up, has_down = row > 0, row < rows - 1
    has_left, has_right = col > 0, col < cols - 1

    load_one = pltpu.make_async_copy(w1_hbm, w1, w_sem.at[0])
    load_two = pltpu.make_async_copy(w2_hbm, w2, w_sem.at[1])
    load_one.start()
    load_two.start()

    barrier = pltpu.get_barrier_semaphore()

    def greet(device_row, first):
        def body(k, carry):
            pl.semaphore_signal(
                barrier, inc=1, device_id=(device_row, lax.rem(col + k, cols)), device_id_type=MESH
            )
            return carry

        lax.fori_loop(first, cols, body, 0)

    greet(row, 1)
    pl.when(has_up)(lambda: greet(row - 1, 0))
    pl.when(has_down)(lambda: greet(row + 1, 0))

    lanes_of = [slice(128 * h, 128 * h + 128) for h in range(ch // 128)]
    for h, part in enumerate(lanes_of):
        x32[h, 2 : tr + 2, 8 : tc + 8, :] = feat[:, :, part].astype(F32)
        st_r[:, :, part] = x32[h, 2 : tr + 2, tc + 6 : tc + 8, :].astype(BF16)
        st_l[:, :, part] = x32[h, 2 : tr + 2, 8:10, :].astype(BF16)
    zero = lambda ref, lo, hi: ref.__setitem__(
        slice(lo, hi), jnp.zeros((hi - lo,) + ref.shape[1:], ref.dtype)
    )
    copies = []
    plan = (
        (feat.at[tr - 2 : tr], rc_u, 1, 0, has_down, has_up, (rc_u, 0, 2)),
        (feat.at[0:1], rc_d, -1, 0, has_up, has_down, (rc_d, 0, 1)),
        (st_r, rc_l.at[2 : tr + 2], 0, 1, has_right, has_left, (rc_l, 2, tr + 2)),
        (st_l, rc_r.at[2 : tr + 2], 0, -1, has_left, has_right, (rc_r, 2, tr + 2)),
        (st_r.at[tr - 2 : tr], rc_l.at[0:2], 1, 1, has_down & has_right, has_up & has_left, (rc_l, 0, 2)),
        (st_r.at[0:1], rc_l.at[tr + 2 : tr + 3], -1, 1, has_up & has_right, has_down & has_left, (rc_l, tr + 2, tr + 3)),
        (st_l.at[tr - 2 : tr], rc_r.at[0:2], 1, -1, has_down & has_left, has_up & has_right, (rc_r, 0, 2)),
        (st_l.at[0:1], rc_r.at[tr + 2 : tr + 3], -1, -1, has_up & has_left, has_down & has_right, (rc_r, tr + 2, tr + 3)),
    )
    for index, (src, dst, dr, dc, sends, gets, hole) in enumerate(plan):
        copy = pltpu.make_async_remote_copy(
            src_ref=src, dst_ref=dst, send_sem=h_send.at[index], recv_sem=h_recv.at[index],
            device_id=(row + dr, col + dc), device_id_type=MESH,
        )
        copies.append(copy)
        pl.when(jnp.logical_not(gets))(functools.partial(zero, *hole))

    reach = cols * (1 + has_up.astype(jnp.int32) + has_down.astype(jnp.int32)) - 1
    pl.semaphore_wait(barrier, reach)
    for copy, item in zip(copies, plan):
        pl.when(item[4])(copy.start)

    width = w3.shape[3]
    quad = 4 * width
    band[...] = jnp.zeros_like(band)
    for b in range(3):
        for a in range(3):
            block = w3[0, a, b]
            for i in range(4):
                at = (i + 3 + a) * width
                band[b, at : at + width, i * width : (i + 1) * width] = block
    bias3 = jnp.concatenate([b3[...]] * 4, axis=1)
    l32[0:8, :] = jnp.zeros((8, l32.shape[1]), F32)
    full = cols * half
    l32[full + 8 : full + 16, :] = jnp.zeros((8, l32.shape[1]), F32)

    @pl.when(jnp.logical_not(has_up))
    def _():
        top[...] = jnp.zeros_like(top)

    @pl.when(jnp.logical_not(has_down))
    def _():
        bot[...] = jnp.zeros_like(bot)

    for copy, item in zip(copies, plan):
        pl.when(item[5])(copy.wait_recv)
    for h, part in enumerate(lanes_of):
        x32[h, 0:2, 8 : tc + 8, :] = rc_u[:, :, part].astype(F32)
        x32[h, tr + 2 : tr + 3, 8 : tc + 8, :] = rc_d[:, :, part].astype(F32)
        x32[h, 0 : tr + 3, 6:8, :] = rc_l[:, :, part].astype(F32)
        x32[h, 0 : tr + 3, tc + 8 : tc + 10, :] = rc_r[:, :, part].astype(F32)

    for j in range(4):
        for r in range(0, tr + 4, 12):
            for h in range(ch // 128):
                taps[r : r + 12, :, j * ch + 128 * h : j * ch + 128 * h + 128] = x32[
                    h, r : r + 12, pl.ds(j + 6, 32, stride=2), :
                ].astype(BF16)

    load_one.wait()
    bias1 = b1[...]
    left_edge = jnp.logical_not(has_left)
    out_ch = w2.shape[3]
    orow = tr // 2
    span = orow * width
    third = half // 3

    def first_layer(first, pairs):
        m = pairs * 64
        for parity in range(2):
            acc = None
            for a in range(3):
                lhs = taps[2 * first + a : 2 * first + a + 2 * pairs, :, parity * ch : (parity + 3) * ch]
                part = dot(lhs.reshape(m, 3 * ch), w1[a].reshape(3 * ch, ch))
                acc = part if acc is None else acc + part
            acc = jnp.maximum(acc + bias1, 0.0)
            if parity == 0:
                spot = lax.broadcasted_iota(jnp.int32, acc.shape, 0)
                acc = jnp.where((lax.rem(spot, 32) == 0) & left_edge, 0.0, acc)
                moved = pltpu.roll(acc, m - 1, 0)
                a2[first : first + pairs, :, :, 2 * ch : 3 * ch] = moved.astype(BF16).reshape(pairs, 2, 32, ch)
            a2[first : first + pairs, :, :, parity * ch : (parity + 1) * ch] = acc.astype(BF16).reshape(
                pairs, 2, 32, ch
            )

    def second_layer(first, count):
        acc = None
        for a in range(3):
            lhs = a2[first + a // 2 : first + a // 2 + count, a % 2].reshape(count * 32, 3 * ch)
            part = dot(lhs, w2[a].reshape(3 * ch, out_ch))
            acc = part if acc is None else acc + part
        l2[first : first + count] = jnp.maximum(acc + b2[...], 0.0).reshape(count, 32, out_ch)

    def pack(p):
        for q in range(orow // 8):
            for g in range(cols):
                piece = jnp.concatenate(
                    [
                        l2[p * orow // 2 + 4 * q + r, 0:half, g * width : (g + 1) * width]
                        for r in range(4)
                    ],
                    axis=1,
                )
                send[p, g, :, q * quad : (q + 1) * quad] = piece.astype(BF16)

    def pack_edge(there, r):
        for g in range(cols):
            pieces = [
                l2[r, third * t : third * (t + 1), g * width : (g + 1) * width] for t in (0, 1, 2, 2)
            ]
            there[g] = jnp.concatenate(pieces, axis=1).astype(BF16)

    def main_copy(p, k):
        d = lax.rem(col + k, cols)
        return pltpu.make_async_remote_copy(
            src_ref=send.at[p, d], dst_ref=main.at[p, col], send_sem=m_send.at[p, k],
            recv_sem=m_recv.at[p, col], device_id=(row, d), device_id_type=MESH,
        )

    def main_arrival(p, k):
        s = lax.rem(col + k, cols)
        return pltpu.make_async_remote_copy(
            src_ref=send.at[p, s], dst_ref=main.at[p, s], send_sem=m_send.at[p, k],
            recv_sem=m_recv.at[p, s], device_id=(row, s), device_id_type=MESH,
        )

    def edge_copy(k, dr):
        d = lax.rem(col + k, cols)
        src, there, ss, rs = (high, top, t_send, t_recv) if dr > 0 else (low, bot, b_send, b_recv)
        return pltpu.make_async_remote_copy(
            src_ref=src.at[d], dst_ref=there.at[col], send_sem=ss.at[k], recv_sem=rs.at[col],
            device_id=(row + dr, d), device_id_type=MESH,
        )

    def edge_arrival(k, dr):
        s = lax.rem(col + k, cols)
        src, there, ss, rs = (high, top, t_send, t_recv) if dr > 0 else (low, bot, b_send, b_recv)
        return pltpu.make_async_remote_copy(
            src_ref=src.at[s], dst_ref=there.at[s], send_sem=ss.at[k], recv_sem=rs.at[s],
            device_id=(row - dr, s), device_id_type=MESH,
        )

    def each(first, act):
        def body(k, carry):
            act(k)
            return carry

        lax.fori_loop(first, cols, body, 0)

    def clear_top():
        a2[0, 0] = jnp.zeros(a2.shape[2:], BF16)

    cut = orow // 2 + 1
    first_layer(0, cut)
    pl.when(jnp.logical_not(has_up))(clear_top)
    load_two.wait()
    second_layer(0, orow // 2)
    pack(0)
    each(1, lambda k: main_copy(0, k).start())
    pack_edge(low, 0)
    pl.when(has_up)(lambda: each(0, lambda k: edge_copy(k, -1).start()))
    first_layer(cut, orow + 1 - cut)
    second_layer(orow // 2, orow // 2)
    pack(1)
    each(1, lambda k: main_copy(1, k).start())
    pack_edge(high, orow - 1)
    pl.when(has_down)(lambda: each(0, lambda k: edge_copy(k, 1).start()))
    main[0, col] = send[0, col]
    main[1, col] = send[1, col]

    end = quad + span
    l32[:, 0 : quad] = jnp.zeros((l32.shape[0], quad), F32)
    l32[:, end : end + quad] = jnp.zeros((l32.shape[0], quad), F32)
    each(1, lambda k: main_arrival(0, k).wait_recv())
    for s in range(cols):
        at = 8 + half * s
        l32[at : at + half, quad : quad + span // 2] = main[0, s].astype(F32)
    pl.when(has_down)(lambda: each(0, lambda k: edge_arrival(k, -1).wait_recv()))
    for s in range(cols):
        for t in range(3):
            at = 8 + half * s + third * t
            l32[at : at + third, end : end + width] = bot[s, :, t * width : (t + 1) * width].astype(F32)
    each(1, lambda k: main_arrival(1, k).wait_recv())
    pl.when(has_up)(lambda: each(0, lambda k: edge_arrival(k, 1).wait_recv()))
    for s in range(cols):
        at = 8 + half * s
        l32[at : at + half, quad + span // 2 : end] = main[1, s].astype(F32)
        for t in range(3):
            at = 8 + half * s + third * t
            l32[at : at + third, quad - width : quad] = top[s, :, t * width : (t + 1) * width].astype(F32)

    shifted = [l32[7 + b : 7 + b + full, :].astype(BF16) for b in range(3)]
    for q in range(orow // 4):
        acc = None
        for b in range(3):
            part = dot(shifted[b][:, q * quad : (q + 3) * quad], band[b])
            acc = part if acc is None else acc + part
        out[4 * q : 4 * q + 4] = (acc + bias3).T.reshape(4, width, full).astype(BF16)

    for copy, item in zip(copies, plan):
        pl.when(item[4])(copy.wait_send)
    each(1, lambda k: main_copy(0, k).wait_send())
    each(1, lambda k: main_copy(1, k).wait_send())
    pl.when(has_down)(lambda: each(0, lambda k: edge_copy(k, 1).wait_send()))
    pl.when(has_up)(lambda: each(0, lambda k: edge_copy(k, -1).wait_send()))


def on_device(rows, cols, features, conv_one, bias_one, conv_two, bias_two, conv_three, bias_three):
    tr, tc, ch = features.shape
    c2 = conv_two.shape[3]
    width = conv_three.shape[3]
    half, orow = tc // 2, tr // 2
    full, span, quad = cols * half, orow * width, 4 * width
    vmem = pl.BlockSpec(memory_space=pltpu.VMEM)
    hbm = pl.BlockSpec(memory_space=pl.ANY)
    dma = pltpu.SemaphoreType.DMA
    return pl.pallas_call(
        functools.partial(kernel, rows, cols),
        out_shape=jax.ShapeDtypeStruct((orow, width, full), BF16),
        in_specs=[vmem, hbm, vmem, hbm, vmem, vmem, vmem],
        out_specs=vmem,
        scratch_shapes=[
            pltpu.VMEM(conv_one.shape, BF16),
            pltpu.VMEM(conv_two.shape, BF16),
            pltpu.VMEM((ch // 128, tr + 4, tc + 24, 128), F32),
            pltpu.VMEM((tr, 2, ch), BF16),
            pltpu.VMEM((tr, 2, ch), BF16),
            pltpu.VMEM((tr + 3, 2, ch), BF16),
            pltpu.VMEM((tr + 3, 2, ch), BF16),
            pltpu.VMEM((2, tc, ch), BF16),
            pltpu.VMEM((1, tc, ch), BF16),
            pltpu.VMEM((tr + 4, 32, 4 * ch), BF16),
            pltpu.VMEM((orow + 1, 2, 32, 3 * ch), BF16),
            pltpu.VMEM((orow, 32, c2), F32),
            pltpu.VMEM((2, cols, half, span // 2), BF16),
            pltpu.VMEM((cols, half // 3, quad), BF16),
            pltpu.VMEM((cols, half // 3, quad), BF16),
            pltpu.VMEM((2, cols, half, span // 2), BF16),
            pltpu.VMEM((cols, half // 3, quad), BF16),
            pltpu.VMEM((cols, half // 3, quad), BF16),
            pltpu.VMEM((full + 16, span + 2 * quad), F32),
            pltpu.VMEM((3, 3 * quad, quad), BF16),
            dma((2,)), dma((8,)), dma((8,)),
            dma((2, cols)), dma((2, cols)), dma((cols,)), dma((cols,)), dma((cols,)), dma((cols,)),
        ],
        compiler_params=pltpu.CompilerParams(
            collective_id=0, has_side_effects=True, vmem_limit_bytes=60 * 1024 * 1024
        ),
    )(
        features, conv_one, bias_one.reshape(1, -1), conv_two, bias_two.reshape(1, -1),
        conv_three, bias_three.reshape(1, -1),
    )


def solution(mesh):
    in_specs = (
        P("row", "col", None),
        P(),
        P(),
        P(),
        P(),
        P("col", None, None, None, None),
        P("col"),
    )
    return jax.shard_map(
        functools.partial(on_device, mesh.shape["row"], mesh.shape["col"]),
        mesh=mesh, in_specs=in_specs, out_specs=P("row", "col", None), check_vma=False,
    )
```

```python
import functools

import jax
import jax.numpy as jnp
from jax import lax
from jax.experimental import pallas as pl
from jax.experimental.pallas import tpu as pltpu
from jax.sharding import PartitionSpec as P

MESH = pl.DeviceIdType.MESH
F32 = jnp.float32
BF16 = jnp.bfloat16


def dot(a, b):
    return jnp.dot(a, b, preferred_element_type=F32)


def kernel(
    rows, cols,
    feat_hbm, w1_hbm, b1_hbm, w2_hbm, b2_hbm, w3_hbm, b3_hbm, out,
    feat, w1, b1, w2, b2, w3, b3, x32, st_l, st_r, rc_l, rc_r, rc_u, rc_d, taps, a2, l2, send, low, high, main, top, bot, l32, band,
    w_sem, h_send, h_recv, m_send, m_recv, t_send, t_recv, b_send, b_recv,
):
    row = lax.axis_index("row")
    col = lax.axis_index("col")
    tr, tc, ch = feat.shape
    half = tc // 2
    has_up, has_down = row > 0, row < rows - 1
    has_left, has_right = col > 0, col < cols - 1

    load_feat, load_w3, load_b3, load_b1, load_one, load_b2, load_two = [
        pltpu.make_async_copy(src, dst, w_sem.at[index])
        for index, (src, dst) in enumerate(
            (
                (feat_hbm, feat), (w3_hbm, w3), (b3_hbm, b3), (b1_hbm, b1),
                (w1_hbm, w1), (b2_hbm, b2), (w2_hbm, w2),
            )
        )
    ]
    load_feat.start()

    barrier = pltpu.get_barrier_semaphore()

    def greet(device_row, first):
        def body(k, carry):
            pl.semaphore_signal(
                barrier, inc=1, device_id=(device_row, lax.rem(col + k, cols)), device_id_type=MESH
            )
            return carry

        lax.fori_loop(first, cols, body, 0)

    greet(row, 1)
    pl.when(has_up)(lambda: greet(row - 1, 0))
    pl.when(has_down)(lambda: greet(row + 1, 0))
    for load in (load_w3, load_b3, load_b1, load_one, load_b2, load_two):
        load.start()
    load_feat.wait()

    lanes_of = [slice(128 * h, 128 * h + 128) for h in range(ch // 128)]
    for h, part in enumerate(lanes_of):
        x32[h, 2 : tr + 2, 8 : tc + 8, :] = feat[:, :, part].astype(F32)
        st_r[:, :, part] = x32[h, 2 : tr + 2, tc + 6 : tc + 8, :].astype(BF16)
        st_l[:, :, part] = x32[h, 2 : tr + 2, 8:10, :].astype(BF16)
    zero = lambda ref, lo, hi: ref.__setitem__(
        slice(lo, hi), jnp.zeros((hi - lo,) + ref.shape[1:], ref.dtype)
    )
    copies = []
    plan = (
        (feat.at[tr - 2 : tr], rc_u, 1, 0, has_down, has_up, (rc_u, 0, 2)),
        (feat.at[0:1], rc_d, -1, 0, has_up, has_down, (rc_d, 0, 1)),
        (st_r, rc_l.at[2 : tr + 2], 0, 1, has_right, has_left, (rc_l, 2, tr + 2)),
        (st_l, rc_r.at[2 : tr + 2], 0, -1, has_left, has_right, (rc_r, 2, tr + 2)),
        (st_r.at[tr - 2 : tr], rc_l.at[0:2], 1, 1, has_down & has_right, has_up & has_left, (rc_l, 0, 2)),
        (st_r.at[0:1], rc_l.at[tr + 2 : tr + 3], -1, 1, has_up & has_right, has_down & has_left, (rc_l, tr + 2, tr + 3)),
        (st_l.at[tr - 2 : tr], rc_r.at[0:2], 1, -1, has_down & has_left, has_up & has_right, (rc_r, 0, 2)),
        (st_l.at[0:1], rc_r.at[tr + 2 : tr + 3], -1, -1, has_up & has_left, has_down & has_right, (rc_r, tr + 2, tr + 3)),
    )
    for index, (src, dst, dr, dc, sends, gets, hole) in enumerate(plan):
        copy = pltpu.make_async_remote_copy(
            src_ref=src, dst_ref=dst, send_sem=h_send.at[index], recv_sem=h_recv.at[index],
            device_id=(row + dr, col + dc), device_id_type=MESH,
        )
        copies.append(copy)
        pl.when(jnp.logical_not(gets))(functools.partial(zero, *hole))

    reach = cols * (1 + has_up.astype(jnp.int32) + has_down.astype(jnp.int32)) - 1
    pl.semaphore_wait(barrier, reach)
    for copy, item in zip(copies, plan):
        pl.when(item[4])(copy.start)

    load_w3.wait()
    load_b3.wait()
    width = w3.shape[3]
    quad = 4 * width
    band[...] = jnp.zeros_like(band)
    for b in range(3):
        for a in range(3):
            block = w3[0, a, b]
            for i in range(4):
                at = (i + 3 + a) * width
                band[b, at : at + width, i * width : (i + 1) * width] = block
    bias3 = jnp.concatenate([b3[...]] * 4, axis=1)
    l32[0:8, :] = jnp.zeros((8, l32.shape[1]), F32)
    full = cols * half
    l32[full + 8 : full + 16, :] = jnp.zeros((8, l32.shape[1]), F32)

    @pl.when(jnp.logical_not(has_up))
    def _():
        top[...] = jnp.zeros_like(top)

    @pl.when(jnp.logical_not(has_down))
    def _():
        bot[...] = jnp.zeros_like(bot)

    for copy, item in zip(copies, plan):
        pl.when(item[5])(copy.wait_recv)
    for h, part in enumerate(lanes_of):
        x32[h, 0:2, 8 : tc + 8, :] = rc_u[:, :, part].astype(F32)
        x32[h, tr + 2 : tr + 3, 8 : tc + 8, :] = rc_d[:, :, part].astype(F32)
        x32[h, 0 : tr + 3, 6:8, :] = rc_l[:, :, part].astype(F32)
        x32[h, 0 : tr + 3, tc + 8 : tc + 10, :] = rc_r[:, :, part].astype(F32)

    for j in range(4):
        for r in range(0, tr + 4, 12):
            for h in range(ch // 128):
                taps[r : r + 12, :, j * ch + 128 * h : j * ch + 128 * h + 128] = x32[
                    h, r : r + 12, pl.ds(j + 6, 32, stride=2), :
                ].astype(BF16)

    load_b1.wait()
    load_one.wait()
    bias1 = b1[...]
    left_edge = jnp.logical_not(has_left)
    out_ch = w2.shape[3]
    orow = tr // 2
    span = orow * width
    third = half // 3

    def first_layer(first, pairs):
        m = pairs * 64
        for parity in range(2):
            acc = None
            for a in range(3):
                lhs = taps[2 * first + a : 2 * first + a + 2 * pairs, :, parity * ch : (parity + 3) * ch]
                part = dot(lhs.reshape(m, 3 * ch), w1[a].reshape(3 * ch, ch))
                acc = part if acc is None else acc + part
            acc = jnp.maximum(acc + bias1, 0.0)
            if parity == 0:
                spot = lax.broadcasted_iota(jnp.int32, acc.shape, 0)
                acc = jnp.where((lax.rem(spot, 32) == 0) & left_edge, 0.0, acc)
                moved = pltpu.roll(acc, m - 1, 0)
                a2[first : first + pairs, :, :, 2 * ch : 3 * ch] = moved.astype(BF16).reshape(pairs, 2, 32, ch)
            a2[first : first + pairs, :, :, parity * ch : (parity + 1) * ch] = acc.astype(BF16).reshape(
                pairs, 2, 32, ch
            )

    def second_layer(first, count):
        acc = None
        for a in range(3):
            lhs = a2[first + a // 2 : first + a // 2 + count, a % 2].reshape(count * 32, 3 * ch)
            part = dot(lhs, w2[a].reshape(3 * ch, out_ch))
            acc = part if acc is None else acc + part
        l2[first : first + count] = jnp.maximum(acc + b2[...], 0.0).reshape(count, 32, out_ch)

    def pack(p):
        for g in range(cols):
            piece = jnp.concatenate(
                [l2[4 * p + r, 0:half, g * width : (g + 1) * width] for r in range(4)], axis=1
            )
            send[p, g] = piece.astype(BF16)

    def pack_edge(there, r):
        for g in range(cols):
            pieces = [
                l2[r, third * t : third * (t + 1), g * width : (g + 1) * width] for t in (0, 1, 2, 2)
            ]
            there[g] = jnp.concatenate(pieces, axis=1).astype(BF16)

    def main_copy(p, d):
        return pltpu.make_async_remote_copy(
            src_ref=send.at[p, d], dst_ref=main.at[p, col], send_sem=m_send.at[p, d],
            recv_sem=m_recv.at[p, col], device_id=(row, d), device_id_type=MESH,
        )

    def main_arrival(p, k):
        s = lax.rem(col + k, cols)
        return pltpu.make_async_remote_copy(
            src_ref=send.at[p, s], dst_ref=main.at[p, s], send_sem=m_send.at[p, s],
            recv_sem=m_recv.at[p, s], device_id=(row, s), device_id_type=MESH,
        )

    def edge_copy(k, dr):
        d = lax.rem(col + k, cols)
        src, there, ss, rs = (high, top, t_send, t_recv) if dr > 0 else (low, bot, b_send, b_recv)
        return pltpu.make_async_remote_copy(
            src_ref=src.at[d], dst_ref=there.at[col], send_sem=ss.at[k], recv_sem=rs.at[col],
            device_id=(row + dr, d), device_id_type=MESH,
        )

    def edge_arrival(k, dr):
        s = lax.rem(col + k, cols)
        src, there, ss, rs = (high, top, t_send, t_recv) if dr > 0 else (low, bot, b_send, b_recv)
        return pltpu.make_async_remote_copy(
            src_ref=src.at[s], dst_ref=there.at[s], send_sem=ss.at[k], recv_sem=rs.at[s],
            device_id=(row - dr, s), device_id_type=MESH,
        )

    def each(first, act):
        def body(k, carry):
            act(k)
            return carry

        lax.fori_loop(first, cols, body, 0)

    def clear_top():
        a2[0, 0] = jnp.zeros(a2.shape[2:], BF16)

    part = cols // 2
    own = col // part

    def send_far(p):
        def body(k, carry):
            main_copy(p, (1 - own) * part + lax.rem(col + k, part)).start()
            return carry

        lax.fori_loop(0, part, body, 0)

    def send_near(p):
        def body(k, carry):
            main_copy(p, own * part + lax.rem(col + k, part)).start()
            return carry

        lax.fori_loop(1, part, body, 0)

    chunks = orow // 4
    for p in range(chunks):
        first_layer(4 * p + (p > 0), 4 + (p == 0))
        if p == 0:
            pl.when(jnp.logical_not(has_up))(clear_top)
            load_b2.wait()
            load_two.wait()
        second_layer(4 * p, 4)
        pack(p)
        send_far(p)
        send_near(p)
        if p == 0:
            pack_edge(low, 0)
            pl.when(has_up)(lambda: each(0, lambda k: edge_copy(k, -1).start()))
        if p == chunks - 1:
            pack_edge(high, orow - 1)
            pl.when(has_down)(lambda: each(0, lambda k: edge_copy(k, 1).start()))
        main[p, col] = send[p, col]

    end = quad + span
    l32[:, 0:quad] = jnp.zeros((l32.shape[0], quad), F32)
    l32[:, end : end + quad] = jnp.zeros((l32.shape[0], quad), F32)
    for p in range(chunks):
        each(1, lambda k: main_arrival(p, k).wait_recv())
        for s in range(cols):
            at = 8 + half * s
            l32[at : at + half, quad * (p + 1) : quad * (p + 2)] = main[p, s].astype(F32)
        if p == 0:
            pl.when(has_down)(lambda: each(0, lambda k: edge_arrival(k, -1).wait_recv()))
            for s in range(cols):
                for t in range(3):
                    at = 8 + half * s + third * t
                    l32[at : at + third, end : end + width] = bot[s, :, t * width : (t + 1) * width].astype(F32)
    pl.when(has_up)(lambda: each(0, lambda k: edge_arrival(k, 1).wait_recv()))
    for s in range(cols):
        for t in range(3):
            at = 8 + half * s + third * t
            l32[at : at + third, quad - width : quad] = top[s, :, t * width : (t + 1) * width].astype(F32)

    shifted = [l32[7 + b : 7 + b + full, :].astype(BF16) for b in range(3)]
    for q in range(orow // 4):
        acc = None
        for b in range(3):
            part = dot(shifted[b][:, q * quad : (q + 3) * quad], band[b])
            acc = part if acc is None else acc + part
        out[4 * q : 4 * q + 4] = (acc + bias3).T.reshape(4, width, full).astype(BF16)

    for copy, item in zip(copies, plan):
        pl.when(item[4])(copy.wait_send)
    for p in range(chunks):
        each(1, lambda k: main_copy(p, lax.rem(col + k, cols)).wait_send())
    pl.when(has_down)(lambda: each(0, lambda k: edge_copy(k, 1).wait_send()))
    pl.when(has_up)(lambda: each(0, lambda k: edge_copy(k, -1).wait_send()))


def on_device(rows, cols, features, conv_one, bias_one, conv_two, bias_two, conv_three, bias_three):
    tr, tc, ch = features.shape
    c2 = conv_two.shape[3]
    width = conv_three.shape[3]
    half, orow = tc // 2, tr // 2
    full, span, quad = cols * half, orow * width, 4 * width
    vmem = pl.BlockSpec(memory_space=pltpu.VMEM)
    hbm = pl.BlockSpec(memory_space=pl.ANY)
    dma = pltpu.SemaphoreType.DMA
    return pl.pallas_call(
        functools.partial(kernel, rows, cols),
        out_shape=jax.ShapeDtypeStruct((orow, width, full), BF16),
        in_specs=[hbm] * 7,
        out_specs=vmem,
        scratch_shapes=[
            pltpu.VMEM(features.shape, BF16),
            pltpu.VMEM(conv_one.shape, BF16),
            pltpu.VMEM((1, ch), F32),
            pltpu.VMEM(conv_two.shape, BF16),
            pltpu.VMEM((1, c2), F32),
            pltpu.VMEM(conv_three.shape, BF16),
            pltpu.VMEM((1, width), F32),
            pltpu.VMEM((ch // 128, tr + 4, tc + 24, 128), F32),
            pltpu.VMEM((tr, 2, ch), BF16),
            pltpu.VMEM((tr, 2, ch), BF16),
            pltpu.VMEM((tr + 3, 2, ch), BF16),
            pltpu.VMEM((tr + 3, 2, ch), BF16),
            pltpu.VMEM((2, tc, ch), BF16),
            pltpu.VMEM((1, tc, ch), BF16),
            pltpu.VMEM((tr + 4, 32, 4 * ch), BF16),
            pltpu.VMEM((orow + 1, 2, 32, 3 * ch), BF16),
            pltpu.VMEM((orow, 32, c2), F32),
            pltpu.VMEM((orow // 4, cols, half, quad), BF16),
            pltpu.VMEM((cols, half // 3, quad), BF16),
            pltpu.VMEM((cols, half // 3, quad), BF16),
            pltpu.VMEM((orow // 4, cols, half, quad), BF16),
            pltpu.VMEM((cols, half // 3, quad), BF16),
            pltpu.VMEM((cols, half // 3, quad), BF16),
            pltpu.VMEM((full + 16, span + 2 * quad), F32),
            pltpu.VMEM((3, 3 * quad, quad), BF16),
            dma((7,)), dma((8,)), dma((8,)),
            dma((orow // 4, cols)), dma((orow // 4, cols)), dma((cols,)), dma((cols,)), dma((cols,)), dma((cols,)),
        ],
        compiler_params=pltpu.CompilerParams(
            collective_id=0, has_side_effects=True, vmem_limit_bytes=60 * 1024 * 1024
        ),
    )(
        features, conv_one, bias_one.reshape(1, -1), conv_two, bias_two.reshape(1, -1),
        conv_three, bias_three.reshape(1, -1),
    )


def solution(mesh):
    in_specs = (
        P("row", "col", None),
        P(),
        P(),
        P(),
        P(),
        P("col", None, None, None, None),
        P("col"),
    )
    return jax.shard_map(
        functools.partial(on_device, mesh.shape["row"], mesh.shape["col"]),
        mesh=mesh, in_specs=in_specs, out_specs=P("row", "col", None), check_vma=False,
    )
```
